32 devices in a mesh: stn: 8 (over z, x), chan: 4 (over y, core).
Axes of the slice: x: 2, y: 2, z: 4, core: 2. Of those that a mesh axis runs over, the one named last changes fastest.
Arguments:
- samples: bfloat16 [64, 17, 2, 8192], P(('stn', 'chan')), may hold values from -6 to 6
- keeper: int32 [8, 8], replicated, may hold values from 0 to 1, as said below
Outputs:
- visibilities: bfloat16 [64, 2, 4096, 40], P('stn', None, 'chan')
The draws below stay inside these ranges and needn't reach their ends.
Inputs may be any that keep to these rules, and one draw needn't show every extreme that they name: keeper[g, g] is 1; for g != h with d = (g - h) mod 8: keeper[g, h] is 1 where 0 < d < 4, 0 where d > 4, and at d = 4 exactly one of keeper[g, h] and keeper[h, g] is 1, which one drawn for each such pair; half of the rows hold 5 ones, the others 5 - 1.
All inputs are finite; a program needn't handle non-finite values.
Results may differ from the reference program's by a relative error of at most 0.0077.
Values may be sent and summed in bfloat16 or wider, within the bound.
A program may use at most 192 MiB of HBM per device.

```python
import math
import jax
import jax.numpy as jnp
from jax import lax

NFFT = 8192
TAPS = 16
STN_DEV = 1
CH_WIN = 1024
DFT_BLOCK = 256
FRAMES = 2
FRAMES_IN = 17
GROUPS = 8
INPUTS = 64
N_STN = 8
N_CHAN = 4


def draw_keeper(key, part):
    middle = GROUPS // 2
    coins = jax.random.randint(jax.random.fold_in(key, 11), (middle,), 0, 2).astype(jnp.int32)
    first = jnp.arange(GROUPS, dtype=jnp.int32)[:, None]
    second = jnp.arange(GROUPS, dtype=jnp.int32)[None, :]
    distance = (first - second) % GROUPS
    coin_row = jnp.take(coins, first % middle)
    lower_wins = (first < second) == (coin_row == 0)
    kept = (distance == 0) | (distance >= 1) & (distance < middle) | (distance == middle) & lower_wins
    return kept.astype(jnp.int32)


def block_levels(rng, dims, pieces, low, largest):
    def one(axis_at, blocks):
        heights = jax.random.uniform(jax.random.fold_in(jax.random.fold_in(rng, 6), axis_at), (blocks,), jnp.float32, low / len(pieces), largest / len(pieces))
        return jnp.repeat(jnp.exp(heights), dims[axis_at] // blocks).reshape((-1,) + (1,) * (len(dims) - axis_at - 1))

    loudness = one(*pieces[0])
    for cut in pieces[1:]:
        loudness = loudness * one(*cut)
    return loudness


def bell_draw(stream_key, dims, scale, limit, split=(), kind=jnp.bfloat16):
    factor_of = block_levels(stream_key, dims, split, -0.22, 0.18) if split else 1.0
    entries = jax.random.normal(stream_key, dims, jnp.float32) * scale * factor_of
    return jnp.minimum(jnp.maximum(entries, -limit), limit).astype(kind)


def setup_inputs(seed: int = 0) -> dict:
    key_list = jax.random.split(jax.random.key(seed), 3)
    return {
        "samples": bell_draw(key_list[0], (INPUTS, FRAMES_IN, 2, NFFT), 1.0, 6.0, ((0, 32),)),
        "keeper": draw_keeper(jax.random.fold_in(key_list[2], 71), 0),
    }


def taps_table():
    pos = jnp.arange(TAPS * NFFT).astype(jnp.float32)
    shifted = (pos + 0.5) / NFFT - TAPS / 2.0
    window = 0.5 - 0.5 * jnp.cos(2.0 * math.pi * (pos + 0.5) / (TAPS * NFFT))
    return (jnp.sinc(shifted) * window).reshape(TAPS, NFFT)

def twiddles(width):
    index_n = jnp.arange(NFFT, dtype=jnp.int32)[:, None]
    index_k = jnp.arange(width, dtype=jnp.int32)[None, :]
    phase = (index_n * index_k % NFFT).astype(jnp.float32) * (2.0 * math.pi / NFFT)
    cosines = jnp.cos(phase).astype(jnp.bfloat16)
    sines = jnp.sin(phase).astype(jnp.bfloat16)
    upper = jnp.concatenate([cosines, -sines], axis=1)
    lower = jnp.concatenate([sines, cosines], axis=1)
    return jnp.concatenate([upper, lower], axis=0)

def rotations(ch_tot, width):
    blocks = ch_tot // width
    index_n = jnp.arange(NFFT, dtype=jnp.int32)[None, :]
    index_b = jnp.arange(blocks, dtype=jnp.int32)[:, None]
    phase = (index_n * index_b * width % NFFT).astype(jnp.float32) * (2.0 * math.pi / NFFT)
    return (jnp.cos(phase), jnp.sin(phase))

def channelise(block, taps, table, cos_rot, sin_rot, ch_tot):
    frames = block.shape[1] - TAPS + 1
    count = block.shape[0]
    width = table.shape[1] // 2
    blocks = ch_tot // width
    total = taps[0] * block[:, 0:frames].astype(jnp.float32)
    for tap in range(1, TAPS):
        total = total + taps[tap] * block[:, tap:tap + frames].astype(jnp.float32)
    real_part = total[:, :, 0][None]
    imag_part = total[:, :, 1][None]
    cosine = cos_rot[:, None, None, :]
    sine = sin_rot[:, None, None, :]
    rot_real = real_part * cosine + imag_part * sine
    rot_imag = imag_part * cosine - real_part * sine
    lhs = jnp.stack([rot_real, rot_imag], axis=3).astype(jnp.bfloat16)
    lhs = lhs.reshape(blocks * count * frames, 2 * NFFT)
    spectrum = jnp.dot(lhs, table, preferred_element_type=jnp.float32) * (1.0 / math.sqrt(NFFT))
    spectrum = spectrum.astype(jnp.bfloat16).reshape(blocks, count, frames, 2, width)
    spectrum = jnp.transpose(spectrum, (1, 0, 4, 3, 2))
    return spectrum.reshape(count, ch_tot, 2, frames)

def correlate(own, others, frames):
    half = others.shape[2] // 2
    turned = jnp.concatenate([-others[:, :, half:], others[:, :, :half]], axis=2)
    rhs = jnp.concatenate([others, turned], axis=0)
    product = lax.dot_general(own.astype(jnp.float32), rhs.astype(jnp.float32), (((2,), (2,)), ((1,), (1,))))
    rows = others.shape[0]
    product = product.reshape(product.shape[0], product.shape[1], 2, rows)
    return jnp.transpose(product, (1, 2, 0, 3)) / frames

def slot_table(keep_rows, keep_slots):
    ranking = (jnp.cumsum(keep_rows, axis=1) - 1).astype(jnp.int32)
    slot_index = jnp.arange(keep_slots, dtype=jnp.int32)
    matched = (keep_rows[:, :, None] == 1) & (ranking[:, :, None] == slot_index[None, None, :])
    column_ids = jnp.arange(keep_rows.shape[1], dtype=jnp.int32)
    slot_column = lax.optimization_barrier(jnp.sum(jnp.where(matched, column_ids[None, :, None], 0), axis=1)).astype(jnp.int32)
    filled = jnp.any(matched, axis=1)
    return (slot_column, filled)

def reference(samples, keeper):
    ch_tot = CH_WIN * N_CHAN
    inputs = samples.shape[0]
    group_in = 2 * STN_DEV * N_CHAN
    keep_slots = N_STN // 2 + 1
    taps = taps_table()
    table = twiddles(DFT_BLOCK)
    cos_rot, sin_rot = rotations(ch_tot, DFT_BLOCK)
    per_block = 2 * STN_DEV
    blocks = samples.reshape(inputs // per_block, per_block, FRAMES_IN, 2, NFFT)
    spectra = lax.map(lambda block: channelise(block, taps, table, cos_rot, sin_rot, ch_tot), blocks)
    spectra = spectra.reshape(inputs, ch_tot, 2 * FRAMES)
    slot_column, filled = slot_table(keeper, keep_slots)
    span_ch = 16

    def one_step(step, result):
        start = (step * span_ch).astype(jnp.int32)
        part = lax.dynamic_slice_in_dim(spectra, start, span_ch, 1)
        tile = correlate(part, part, FRAMES)
        tile = tile.reshape(N_STN, group_in, 2, span_ch, N_STN, group_in)
        picked = jnp.take_along_axis(tile, slot_column[:, None, None, None, :, None], axis=4)
        picked = jnp.where(filled[:, None, None, None, :, None], picked, jnp.zeros((), jnp.float32))
        picked = picked.reshape(inputs, 2, span_ch, keep_slots * group_in).astype(jnp.bfloat16)
        return lax.dynamic_update_slice_in_dim(result, picked, start, 2)
    result = jnp.zeros((inputs, 2, ch_tot, keep_slots * group_in), jnp.bfloat16)
    return lax.fori_loop(0, ch_tot // span_ch, one_step, result)
```

```python
import functools
import math

import jax
import jax.numpy as jnp
import numpy as np
from jax import lax
from jax.experimental import pallas as pl
from jax.experimental.pallas import tpu as pltpu
from jax.sharding import PartitionSpec as P

TAPS = 16
LANES = 128
CH_WIN = 1024
HIGH = lax.Precision.HIGHEST


def tables(nfft, n_k2):
    n_1 = nfft // LANES
    pos = np.arange(TAPS * nfft, dtype=np.float64)
    window = 0.5 - 0.5 * np.cos(2.0 * np.pi * (pos + 0.5) / (TAPS * nfft))
    taps = np.sinc((pos + 0.5) / nfft - TAPS / 2.0) * window
    taps = np.repeat(taps.reshape(TAPS, n_1, LANES), 2, axis=1)
    k_1 = np.arange(n_1)
    n_2 = np.arange(LANES)
    angle = 2.0 * np.pi * (k_1[:, None] * k_1[None, :] % n_1) / n_1
    cosine, sine = np.cos(angle), np.sin(angle)
    first = np.zeros((2, n_1, n_1, 2))
    first[0, :, :, 0] = cosine
    first[0, :, :, 1] = sine
    first[1, :, :, 0] = -sine
    first[1, :, :, 1] = cosine
    first = first.reshape(2 * n_1, 2 * n_1)
    angle = 2.0 * np.pi * (n_2[:, None] * k_1[None, :] % nfft) / nfft
    scale = 1.0 / math.sqrt(nfft)
    turn_c = np.concatenate([np.cos(angle), np.cos(angle)], axis=1) * scale
    turn_s = np.concatenate([np.sin(angle), -np.sin(angle)], axis=1) * scale
    k_2 = np.concatenate([np.arange(0, n_k2, 2), np.arange(1, n_k2, 2)])
    angle = 2.0 * np.pi * (k_2[:, None] * n_2[None, :] % LANES) / LANES
    second = np.concatenate([np.cos(angle), np.sin(angle)], axis=1)
    return [np.asarray(a, np.float32) for a in (taps, first, turn_c, turn_s, second)]


def filter_rows(x_ref, taps_ref, held, inputs, frames):
    rows = taps_ref.shape[1]
    chunk = 16
    for start in range(0, rows, chunk):
        part = slice(start, start + chunk)
        for i in range(inputs):
            totals = [None] * frames
            for step in range(TAPS + frames - 1):
                value = x_ref[i, step, part, :].astype(jnp.float32)
                for f in range(frames):
                    if 0 <= step - f < TAPS:
                        term = value * taps_ref[step - f, part, :]
                        totals[f] = term if totals[f] is None else totals[f] + term
            for f in range(frames):
                seq = i * frames + f
                held[part, seq * LANES : (seq + 1) * LANES] = totals[f]


def transform(held, first_ref, turn_c_ref, turn_s_ref, second_ref, seqs):
    half = LANES // 2
    stage = jnp.dot(first_ref[...], held[...], precision=HIGH, preferred_element_type=jnp.float32)
    lane = lax.broadcasted_iota(jnp.int32, (LANES, LANES), 1)
    sign = jnp.where(lane < half, 1.0, -1.0)
    tops, lows = [], []
    for seq in range(seqs):
        turned = stage[:, seq * LANES : (seq + 1) * LANES].T
        turned = turned * turn_c_ref[...] + pltpu.roll(turned, half, 1) * turn_s_ref[...]
        tops.append(turned)
        lows.append(pltpu.roll(turned, half, 1) * sign)
    rhs = jnp.concatenate([jnp.concatenate(tops, axis=1), jnp.concatenate(lows, axis=1)], axis=0)
    spectra = jnp.dot(second_ref[...], rhs, precision=HIGH, preferred_element_type=jnp.float32)
    tiles = spectra.shape[0] // 2
    low_lane = lax.broadcasted_iota(jnp.int32, (tiles, LANES), 1) < half
    planes = []
    for seq in range(seqs):
        even = spectra[:tiles, seq * LANES : (seq + 1) * LANES]
        odd = spectra[tiles:, seq * LANES : (seq + 1) * LANES]
        real = jnp.where(low_lane, even, pltpu.roll(odd, half, 1))
        imag = jnp.where(low_lane, pltpu.roll(even, half, 1), odd)
        planes.append((real, imag))
    return planes


def channel_kernel(x_ref, taps_ref, first_ref, turn_c_ref, turn_s_ref, second_ref, out_ref, held):
    inputs, frames = out_ref.shape[1], out_ref.shape[2]
    n_chan, tiles = out_ref.shape[0], out_ref.shape[4]
    filter_rows(x_ref, taps_ref, held, inputs, frames)
    planes = transform(held, first_ref, turn_c_ref, turn_s_ref, second_ref, inputs * frames)
    for i in range(inputs):
        for f in range(frames):
            for p in range(2):
                plane = planes[i * frames + f][p].astype(jnp.bfloat16)
                for d in range(n_chan):
                    out_ref[d, i, f, p] = plane[d * tiles : (d + 1) * tiles]


def channelise(samples, n_chan):
    inputs, frames_in, _, nfft = samples.shape
    frames = frames_in - TAPS + 1
    tiles = CH_WIN // LANES
    n_1 = nfft // LANES
    consts = tables(nfft, CH_WIN * n_chan // n_1)
    x = samples.reshape(inputs, frames_in, 2, n_1, LANES)
    x = jnp.transpose(x, (0, 1, 3, 2, 4)).reshape(inputs, frames_in, 2 * n_1, LANES)
    return pl.pallas_call(
        channel_kernel,
        out_shape=jax.ShapeDtypeStruct((n_chan, inputs, frames, 2, tiles, LANES), jnp.bfloat16),
        in_specs=[pl.BlockSpec(memory_space=pltpu.VMEM)] * 6,
        out_specs=pl.BlockSpec(memory_space=pltpu.VMEM),
        scratch_shapes=[pltpu.VMEM((2 * n_1, inputs * frames * LANES), jnp.float32)],
        name="channelise",
    )(x, *consts)


def correlate_kernel(width, dist_ref, fill_ref, parts_ref, out_ref, rhs):
    step = pl.program_id(0)
    _, inputs, frames, _, tiles, _ = parts_ref.shape
    slots = dist_ref.shape[0]

    @pl.when(step == 0)
    def _():
        rhs[...] = jnp.zeros_like(rhs)
        for s in range(slots):
            d = dist_ref[s]
            gain = fill_ref[s]
            for f in range(frames):
                block = []
                for p in range(2):
                    value = parts_ref[d, :, f, p].astype(jnp.float32) * gain
                    block.append(jnp.transpose(value, (1, 0, 2)))
                real, imag = block
                real_col = slice(2 * f * LANES, (2 * f + 1) * LANES)
                imag_col = slice((2 * f + 1) * LANES, (2 * f + 2) * LANES)
                top = slice(s * inputs, (s + 1) * inputs)
                low = slice(width + s * inputs, width + (s + 1) * inputs)
                rhs[:, top, real_col] = real.astype(jnp.bfloat16)
                rhs[:, top, imag_col] = imag.astype(jnp.bfloat16)
                rhs[:, low, real_col] = (-imag).astype(jnp.bfloat16)
                rhs[:, low, imag_col] = real.astype(jnp.bfloat16)

    row_id = lax.broadcasted_iota(jnp.int32, (LANES, LANES), 0)
    col_id = lax.broadcasted_iota(jnp.int32, (LANES, LANES), 1)
    eye = jnp.where(row_id == col_id, 1.0, 0.0).astype(jnp.bfloat16)
    sub_id = lax.broadcasted_iota(jnp.int32, (tiles, LANES), 0)
    weights = rhs[step]
    for i in range(inputs):
        diags = []
        for f in range(frames):
            for p in range(2):
                rows = parts_ref[0, i, f, p].astype(jnp.float32)
                row = jnp.sum(jnp.where(sub_id == step, rows, 0.0), axis=0, keepdims=True)
                wide = jnp.broadcast_to(row, (LANES, LANES)).astype(jnp.bfloat16)
                diags.append(wide * eye)
        product = lax.dot_general(
            jnp.concatenate(diags, axis=1),
            weights,
            (((1,), (1,)), ((), ())),
            preferred_element_type=jnp.float32,
        )
        cols = out_ref.shape[3]
        out_ref[i, 0] = product[:, :cols].astype(jnp.bfloat16)
        out_ref[i, 1] = product[:, width : width + cols].astype(jnp.bfloat16)


def correlate(parts, dist, gain):
    _, inputs, frames, _, tiles, _ = parts.shape
    slots = dist.shape[0]
    cols = slots * inputs
    width = -(-cols // LANES) * LANES
    return pl.pallas_call(
        functools.partial(correlate_kernel, width),
        out_shape=jax.ShapeDtypeStruct((inputs, 2, tiles * LANES, cols), jnp.bfloat16),
        grid=(tiles,),
        in_specs=[
            pl.BlockSpec(memory_space=pltpu.SMEM),
            pl.BlockSpec(memory_space=pltpu.SMEM),
            pl.BlockSpec(parts.shape, lambda t: (0,) * 6),
        ],
        out_specs=pl.BlockSpec((inputs, 2, LANES, cols), lambda t: (0, 0, t, 0)),
        scratch_shapes=[pltpu.VMEM((tiles, 2 * width, 2 * frames * LANES), jnp.bfloat16)],
        name="correlate",
    )(dist, gain, parts)


def slot_table(keep_row, keep_slots):
    ranking = jnp.cumsum(keep_row) - 1
    slot_index = jnp.arange(keep_slots, dtype=jnp.int32)
    matched = (keep_row[:, None] == 1) & (ranking[:, None] == slot_index[None, :])
    column_ids = jnp.arange(keep_row.shape[0], dtype=jnp.int32)
    slot_column = jnp.sum(jnp.where(matched, column_ids[:, None], 0), axis=0)
    filled = jnp.any(matched, axis=0)
    return slot_column, filled


def from_behind(value, axis, by):
    devices = lax.axis_size(axis)
    return lax.ppermute(value, axis, [(i, (i + by) % devices) for i in range(devices)])


def per_device(samples, keeper):
    n_chan = lax.axis_size("chan")
    n_stn = lax.axis_size("stn")
    half = n_stn // 2
    frames = samples.shape[1] - TAPS + 1
    group = lax.axis_index("stn")
    slot_column, filled = slot_table(jnp.take(keeper, group, axis=0), half + 1)
    dist = jnp.minimum((group - slot_column) % n_stn, half).astype(jnp.int32)
    gain = jnp.where(filled, 1.0 / frames, 0.0).astype(jnp.float32)

    spectrum = channelise(samples, n_chan)
    own = lax.all_to_all(spectrum, "chan", split_axis=0, concat_axis=0, tiled=True)
    own = own.reshape((own.shape[0] * own.shape[1],) + own.shape[2:])
    stacked = own[None]
    stride = 1
    while stride < half:
        moved = from_behind(stacked, "stn", stride)
        stacked = jnp.concatenate([stacked, moved], axis=0)
        stride = stride * 2
    far_group = from_behind(own, "stn", half)
    parts = jnp.concatenate([stacked, far_group[None]], axis=0)
    return correlate(parts, dist, gain)


def solution(mesh):
    placed = (P(("stn", "chan"), None, None, None), P())
    return jax.shard_map(
        per_device,
        mesh=mesh,
        in_specs=placed,
        out_specs=P("stn", None, "chan", None),
        check_vma=False,
    )
```

```python
import math

import jax
import jax.numpy as jnp
import numpy as np
from jax import lax
from jax.experimental import pallas as pl
from jax.experimental.pallas import tpu as pltpu
from jax.sharding import PartitionSpec as P

TAPS = 16
LANES = 128
CH_WIN = 1024
HIGH = lax.Precision.HIGHEST
OUT_SPACE = pl.ANY


def tables(nfft, n_k2):
    n_1 = nfft // LANES
    pos = np.arange(TAPS * nfft, dtype=np.float64)
    window = 0.5 - 0.5 * np.cos(2.0 * np.pi * (pos + 0.5) / (TAPS * nfft))
    taps = np.sinc((pos + 0.5) / nfft - TAPS / 2.0) * window
    taps = np.repeat(taps.reshape(TAPS, n_1, LANES), 2, axis=1)
    k_1 = np.arange(n_1)
    n_2 = np.arange(LANES)
    angle = 2.0 * np.pi * (k_1[:, None] * k_1[None, :] % n_1) / n_1
    cosine, sine = np.cos(angle), np.sin(angle)
    first = np.zeros((2, n_1, n_1, 2))
    first[0, :, :, 0] = cosine
    first[0, :, :, 1] = sine
    first[1, :, :, 0] = -sine
    first[1, :, :, 1] = cosine
    first = first.reshape(2 * n_1, 2 * n_1)
    angle = 2.0 * np.pi * (n_2[:, None] * k_1[None, :] % nfft) / nfft
    scale = 1.0 / math.sqrt(nfft)
    turn_c = np.concatenate([np.cos(angle), np.cos(angle)], axis=1) * scale
    turn_s = np.concatenate([np.sin(angle), -np.sin(angle)], axis=1) * scale
    k_2 = np.concatenate([np.arange(0, n_k2, 2), np.arange(1, n_k2, 2)])
    angle = 2.0 * np.pi * (k_2[:, None] * n_2[None, :] % LANES) / LANES
    second = np.concatenate([np.cos(angle), np.sin(angle)], axis=1)
    return [np.asarray(a, np.float32) for a in (taps, first, turn_c, turn_s, second)]


def filter_rows(x_ref, taps_ref, held, inputs, frames):
    rows = taps_ref.shape[1]
    chunk = 16
    for start in range(0, rows, chunk):
        part = slice(start, start + chunk)
        for i in range(inputs):
            totals = [None] * frames
            for step in range(TAPS + frames - 1):
                value = x_ref[i, step, part, :].astype(jnp.float32)
                for f in range(frames):
                    if 0 <= step - f < TAPS:
                        term = value * taps_ref[step - f, part, :]
                        totals[f] = term if totals[f] is None else totals[f] + term
            for f in range(frames):
                seq = i * frames + f
                held[part, seq * LANES : (seq + 1) * LANES] = totals[f]


def transform(held, first_ref, turn_c_ref, turn_s_ref, second_ref, seqs):
    half = LANES // 2
    stage = jnp.dot(first_ref[...], held[...], precision=HIGH, preferred_element_type=jnp.float32)
    lane = lax.broadcasted_iota(jnp.int32, (LANES, LANES), 1)
    sign = jnp.where(lane < half, 1.0, -1.0)
    tops, lows = [], []
    for seq in range(seqs):
        turned = stage[:, seq * LANES : (seq + 1) * LANES].T
        turned = turned * turn_c_ref[...] + pltpu.roll(turned, half, 1) * turn_s_ref[...]
        tops.append(turned)
        lows.append(pltpu.roll(turned, half, 1) * sign)
    rhs = jnp.concatenate([jnp.concatenate(tops, axis=1), jnp.concatenate(lows, axis=1)], axis=0)
    spectra = jnp.dot(second_ref[...], rhs, precision=HIGH, preferred_element_type=jnp.float32)
    tiles = spectra.shape[0] // 2
    low_lane = lax.broadcasted_iota(jnp.int32, (tiles, LANES), 1) < half
    planes = []
    for seq in range(seqs):
        even = spectra[:tiles, seq * LANES : (seq + 1) * LANES]
        odd = spectra[tiles:, seq * LANES : (seq + 1) * LANES]
        real = jnp.where(low_lane, even, pltpu.roll(odd, half, 1))
        imag = jnp.where(low_lane, pltpu.roll(even, half, 1), odd)
        planes.append((real, imag))
    return planes


def send_kernel(
    x_ref, taps_ref, first_ref, turn_c_ref, turn_s_ref, second_ref, parts_ref, held, mine, here_sem, send_sem, pass_sem, recv_sem
):
    n_chan, inputs, frames, _, tiles, _ = mine.shape
    n_stn = lax.axis_size("stn")
    hops = (parts_ref.shape[0] - 1) // 2
    stn = lax.axis_index("stn")
    chan = lax.axis_index("chan")
    odd = lax.rem(stn, 2)
    pair = stn + 1 - 2 * odd

    barrier = pltpu.get_barrier_semaphore()
    for j in range(hops + 1):
        for step in range(n_chan):
            if j or step:
                there = (lax.rem(stn + n_stn - 2 * j, n_stn), lax.rem(chan + step, n_chan))
                pl.semaphore_signal(barrier, inc=1, device_id=there, device_id_type=pl.DeviceIdType.MESH)
    pl.semaphore_signal(barrier, inc=1, device_id=(pair, chan), device_id_type=pl.DeviceIdType.MESH)

    filter_rows(x_ref, taps_ref, held, inputs, frames)
    planes = transform(held, first_ref, turn_c_ref, turn_s_ref, second_ref, inputs * frames)
    for i in range(inputs):
        for f in range(frames):
            for p in range(2):
                plane = planes[i * frames + f][p].astype(jnp.bfloat16)
                for d in range(n_chan):
                    mine[d, i, f, p] = plane[d * tiles : (d + 1) * tiles]
    pl.semaphore_wait(barrier, (hops + 1) * n_chan)

    def direct(j, step):
        to = lax.rem(chan + step, n_chan)
        return pltpu.make_async_remote_copy(
            src_ref=mine.at[to],
            dst_ref=parts_ref.at[2 * j, chan],
            send_sem=send_sem.at[j, step],
            recv_sem=recv_sem.at[2 * j, chan],
            device_id=(lax.rem(stn + 2 * j, n_stn), to),
            device_id_type=pl.DeviceIdType.MESH,
        )

    def arrival(distance, origin):
        return pltpu.make_async_remote_copy(
            src_ref=mine.at[0],
            dst_ref=parts_ref.at[distance, origin],
            send_sem=send_sem.at[0, 0],
            recv_sem=recv_sem.at[distance, origin],
            device_id=(pair, chan),
            device_id_type=pl.DeviceIdType.MESH,
        )

    def passed(j, step):
        origin = lax.rem(chan + step, n_chan)
        return pltpu.make_async_remote_copy(
            src_ref=parts_ref.at[2 * (j + odd), origin],
            dst_ref=parts_ref.at[2 * j + 1, origin],
            send_sem=pass_sem.at[j, step],
            recv_sem=recv_sem.at[2 * j + 1, origin],
            device_id=(pair, chan),
            device_id_type=pl.DeviceIdType.MESH,
        )

    keep = pltpu.make_async_copy(mine.at[chan], parts_ref.at[0, chan], here_sem)
    keep.start()
    for step in range(n_chan):
        for j in range(hops, -1, -1):
            if j or step:
                direct(j, step).start()
    keep.wait()
    for j in range(hops + 1):
        for step in range(n_chan):
            if j or step:
                arrival(2 * j, lax.rem(chan + n_chan - step, n_chan)).wait_recv()
        first = j == 0
        last = j == hops

        @pl.when(odd == 0)
        def _():
            if not last:
                for step in range(n_chan):
                    passed(j, step).start()

        @pl.when(odd == 1)
        def _():
            if not first:
                for step in range(n_chan):
                    passed(j - 1, step).start()

    for j in range(hops):
        for step in range(n_chan):
            arrival(2 * j + 1, lax.rem(chan + step, n_chan)).wait_recv()
            passed(j, step).wait_send()
    for j in range(hops + 1):
        for step in range(n_chan):
            if j or step:
                direct(j, step).wait_send()


def channelise(samples, n_chan, half):
    inputs, frames_in, _, nfft = samples.shape
    frames = frames_in - TAPS + 1
    tiles = CH_WIN // LANES
    n_1 = nfft // LANES
    consts = tables(nfft, CH_WIN * n_chan // n_1)
    x = samples.reshape(inputs, frames_in, 2, n_1, LANES)
    x = jnp.transpose(x, (0, 1, 3, 2, 4)).reshape(inputs, frames_in, 2 * n_1, LANES)
    piece = (n_chan, inputs, frames, 2, tiles, LANES)
    return pl.pallas_call(
        send_kernel,
        out_shape=jax.ShapeDtypeStruct((half + 1,) + piece, jnp.bfloat16),
        in_specs=[pl.BlockSpec(memory_space=pltpu.VMEM)] * 6,
        out_specs=pl.BlockSpec(memory_space=OUT_SPACE),
        scratch_shapes=[
            pltpu.VMEM((2 * n_1, inputs * frames * LANES), jnp.float32),
            pltpu.VMEM(piece, jnp.bfloat16),
            pltpu.SemaphoreType.DMA,
            pltpu.SemaphoreType.DMA((half // 2 + 1, n_chan)),
            pltpu.SemaphoreType.DMA((half // 2, n_chan)),
            pltpu.SemaphoreType.DMA((half + 1, n_chan)),
        ],
        compiler_params=pltpu.CompilerParams(collective_id=0, has_side_effects=True),
        name="channelise",
    )(x, *consts)


def correlate_kernel(keeper_ref, parts_ref, out_ref, own, others, dist, gain):
    step = pl.program_id(0)
    _, n_chan, pieces, frames, _, tiles, _ = parts_ref.shape
    inputs = n_chan * pieces
    slots = parts_ref.shape[0]
    n_stn = keeper_ref.shape[0]

    @pl.when(step == 0)
    def _():
        group = lax.axis_index("stn")
        for s in range(slots):
            dist[s] = 0
            gain[s] = jnp.float32(0.0)

        def place(h, rank):
            kept = keeper_ref[group, h] == 1

            @pl.when(kept & (rank < slots))
            def _():
                dist[rank] = jnp.minimum(lax.rem(group + n_stn - h, n_stn), slots - 1)
                gain[rank] = jnp.float32(1.0 / frames)

            return rank + kept.astype(jnp.int32)

        lax.fori_loop(0, n_stn, place, jnp.int32(0))

        for f in range(frames):
            for p in range(2):
                value = parts_ref[0, :, :, f, p].astype(jnp.float32).reshape(inputs, tiles, LANES)
                own[f, p] = jnp.transpose(value, (1, 0, 2))
                for s in range(slots):
                    value = parts_ref[dist[s], :, :, f, p].astype(jnp.float32) * gain[s]
                    value = value.reshape(inputs, tiles, LANES)
                    others[f, p, s] = jnp.transpose(value, (1, 0, 2))

    for t in range(tiles):
        rows = []
        for i in range(pieces):
            rows.append([
                [jnp.broadcast_to(own[f, p, t, pl.ds(step * pieces + i, 1), :], (inputs, LANES)) for p in range(2)]
                for f in range(frames)
            ])
        for s in range(slots):
            block = [[others[f, p, s, t] for p in range(2)] for f in range(frames)]
            for i in range(pieces):
                real, imag = 0.0, 0.0
                for f in range(frames):
                    a_re, a_im = rows[i][f]
                    b_re, b_im = block[f]
                    real = real + (a_re * b_re + a_im * b_im)
                    imag = imag + (a_im * b_re - a_re * b_im)
                top = slice(s * inputs, (s + 1) * inputs)
                col = slice(t * LANES, (t + 1) * LANES)
                out_ref[i, 0, top, col] = real.astype(jnp.bfloat16)
                out_ref[i, 1, top, col] = imag.astype(jnp.bfloat16)


def correlate(keeper, parts):
    slots, n_chan, pieces, frames, _, tiles, _ = parts.shape
    inputs = n_chan * pieces
    out = pl.pallas_call(
        correlate_kernel,
        out_shape=jax.ShapeDtypeStruct((inputs, 2, slots * inputs, tiles * LANES), jnp.bfloat16),
        grid=(n_chan,),
        in_specs=[
            pl.BlockSpec(memory_space=pltpu.SMEM),
            pl.BlockSpec(parts.shape, lambda t: (0,) * 7),
        ],
        out_specs=pl.BlockSpec((pieces, 2, slots * inputs, tiles * LANES), lambda t: (t, 0, 0, 0)),
        scratch_shapes=[
            pltpu.VMEM((frames, 2, tiles, inputs, LANES), jnp.float32),
            pltpu.VMEM((frames, 2, slots, tiles, inputs, LANES), jnp.float32),
            pltpu.SMEM((slots,), jnp.int32),
            pltpu.SMEM((slots,), jnp.float32),
        ],
        name="correlate",
    )(keeper, parts)
    return jnp.transpose(out, (0, 1, 3, 2))


def per_device(samples, keeper):
    half = lax.axis_size("stn") // 2
    return correlate(keeper, channelise(samples, lax.axis_size("chan"), half))


def solution(mesh):
    placed = (P(("stn", "chan"), None, None, None), P())
    return jax.shard_map(
        per_device,
        mesh=mesh,
        in_specs=placed,
        out_specs=P("stn", None, "chan", None),
        check_vma=False,
    )
```

```python
import math

import jax
import jax.numpy as jnp
import numpy as np
from jax import lax
from jax.experimental import pallas as pl
from jax.experimental.pallas import tpu as pltpu
from jax.sharding import PartitionSpec as P

TAPS = 16
LANES = 128
CH_WIN = 1024
HIGH = lax.Precision.HIGHEST
OUT_SPACE = pl.ANY


def tables(nfft, n_k2):
    n_1 = nfft // LANES
    pos = np.arange(TAPS * nfft, dtype=np.float64)
    window = 0.5 - 0.5 * np.cos(2.0 * np.pi * (pos + 0.5) / (TAPS * nfft))
    taps = np.sinc((pos + 0.5) / nfft - TAPS / 2.0) * window
    taps = np.repeat(taps.reshape(TAPS, n_1, LANES), 2, axis=1)
    k_1 = np.arange(n_1)
    n_2 = np.arange(LANES)
    angle = 2.0 * np.pi * (k_1[:, None] * k_1[None, :] % n_1) / n_1
    cosine, sine = np.cos(angle), np.sin(angle)
    first = np.zeros((2, n_1, n_1, 2))
    first[0, :, :, 0] = cosine
    first[0, :, :, 1] = sine
    first[1, :, :, 0] = -sine
    first[1, :, :, 1] = cosine
    first = first.reshape(2 * n_1, 2 * n_1)
    angle = 2.0 * np.pi * (n_2[:, None] * k_1[None, :] % nfft) / nfft
    scale = 1.0 / math.sqrt(nfft)
    turn_c = np.concatenate([np.cos(angle), np.cos(angle)], axis=1) * scale
    turn_s = np.concatenate([np.sin(angle), -np.sin(angle)], axis=1) * scale
    k_2 = np.concatenate([np.arange(0, n_k2, 2), np.arange(1, n_k2, 2)])
    angle = 2.0 * np.pi * (k_2[:, None] * n_2[None, :] % LANES) / LANES
    second = np.concatenate([np.cos(angle), np.sin(angle)], axis=1)
    return [np.asarray(a, np.float32) for a in (taps, first, turn_c, turn_s, second)]


def filter_rows(x_ref, taps_ref, held, i, frames):
    rows = taps_ref.shape[1]
    chunk = 16
    for start in range(0, rows, chunk):
        part = slice(start, start + chunk)
        totals = [None] * frames
        for step in range(TAPS + frames - 1):
            value = x_ref[i, step, part, :].astype(jnp.float32)
            for f in range(frames):
                if 0 <= step - f < TAPS:
                    term = value * taps_ref[step - f, part, :]
                    totals[f] = term if totals[f] is None else totals[f] + term
        for f in range(frames):
            held[part, f * LANES : (f + 1) * LANES] = totals[f]


def transform(held, first_ref, turn_c_ref, turn_s_ref, second_ref, seqs):
    half = LANES // 2
    stage = jnp.dot(first_ref[...], held[...], precision=HIGH, preferred_element_type=jnp.float32)
    lane = lax.broadcasted_iota(jnp.int32, (LANES, LANES), 1)
    sign = jnp.where(lane < half, 1.0, -1.0)
    tops, lows = [], []
    for seq in range(seqs):
        turned = stage[:, seq * LANES : (seq + 1) * LANES].T
        turned = turned * turn_c_ref[...] + pltpu.roll(turned, half, 1) * turn_s_ref[...]
        tops.append(turned)
        lows.append(pltpu.roll(turned, half, 1) * sign)
    rhs = jnp.concatenate([jnp.concatenate(tops, axis=1), jnp.concatenate(lows, axis=1)], axis=0)
    spectra = jnp.dot(second_ref[...], rhs, precision=HIGH, preferred_element_type=jnp.float32)
    tiles = spectra.shape[0] // 2
    low_lane = lax.broadcasted_iota(jnp.int32, (tiles, LANES), 1) < half
    planes = []
    for seq in range(seqs):
        even = spectra[:tiles, seq * LANES : (seq + 1) * LANES]
        odd = spectra[tiles:, seq * LANES : (seq + 1) * LANES]
        real = jnp.where(low_lane, even, pltpu.roll(odd, half, 1))
        imag = jnp.where(low_lane, pltpu.roll(even, half, 1), odd)
        planes.append((real, imag))
    return planes


def send_kernel(
    x_ref, taps_ref, first_ref, turn_c_ref, turn_s_ref, second_ref, parts_ref, x, taps, held, mine, load_sem, here_sem, send_sem, pass_sem, recv_sem
):
    n_chan, inputs, frames, _, tiles, _ = mine.shape
    n_stn = lax.axis_size("stn")
    hops = (parts_ref.shape[0] - 1) // 2
    stn = lax.axis_index("stn")
    chan = lax.axis_index("chan")
    odd = lax.rem(stn, 2)
    pair = stn + 1 - 2 * odd

    barrier = pltpu.get_barrier_semaphore()
    for j in range(hops + 1):
        for step in range(n_chan):
            if j or step:
                there = (lax.rem(stn + n_stn - 2 * j, n_stn), lax.rem(chan + step, n_chan))
                pl.semaphore_signal(barrier, inc=1, device_id=there, device_id_type=pl.DeviceIdType.MESH)
    pl.semaphore_signal(barrier, inc=1, device_id=(pair, chan), device_id_type=pl.DeviceIdType.MESH)

    def place(turn):
        return turn + odd * (hops - 2 * turn)

    def direct(j, step, src, dst):
        return pltpu.make_async_remote_copy(
            src_ref=src,
            dst_ref=dst,
            send_sem=send_sem.at[j, step],
            recv_sem=recv_sem.at[2 * j, chan],
            device_id=(lax.rem(stn + 2 * j, n_stn), lax.rem(chan + step, n_chan)),
            device_id_type=pl.DeviceIdType.MESH,
        )

    def arrival(distance, origin):
        return pltpu.make_async_remote_copy(
            src_ref=mine.at[0],
            dst_ref=parts_ref.at[distance, origin],
            send_sem=send_sem.at[0, 0],
            recv_sem=recv_sem.at[distance, origin],
            device_id=(pair, chan),
            device_id_type=pl.DeviceIdType.MESH,
        )

    def passed(turn, step):
        origin = lax.rem(chan + n_chan - step, n_chan)
        j = place(turn)
        there = 2 * j + 1 - 2 * odd
        return pltpu.make_async_remote_copy(
            src_ref=parts_ref.at[2 * j, origin],
            dst_ref=parts_ref.at[there, origin],
            send_sem=pass_sem.at[turn, step],
            recv_sem=recv_sem.at[there, origin],
            device_id=(pair, chan),
            device_id_type=pl.DeviceIdType.MESH,
        )

    keep = pltpu.make_async_copy(mine.at[chan], parts_ref.at[0, chan], here_sem)
    copies = [pltpu.make_async_copy(taps_ref, taps, load_sem.at[inputs])]
    copies += [pltpu.make_async_copy(x_ref.at[i], x.at[i], load_sem.at[i]) for i in range(inputs)]
    for copy in copies:
        copy.start()
    copies[0].wait()
    for i in range(inputs):
        copies[i + 1].wait()
        filter_rows(x, taps, held, i, frames)
        planes = transform(held, first_ref, turn_c_ref, turn_s_ref, second_ref, frames)
        for f in range(frames):
            for p in range(2):
                plane = planes[f][p].astype(jnp.bfloat16)
                for d in range(n_chan):
                    mine[d, i, f, p] = plane[d * tiles : (d + 1) * tiles]
        if i == 0:
            pl.semaphore_wait(barrier, (hops + 1) * n_chan)
        for turn in range(hops + 1):
            j = place(turn)
            for step in range(n_chan):
                to = lax.rem(chan + step, n_chan)
                copy = direct(j, step, mine.at[to, i], parts_ref.at[2 * j, chan, i])
                if step:
                    copy.start()
                else:
                    pl.when(j != 0)(copy.start)
    keep.start()

    for turn in range(hops + 1):
        j = place(turn)
        for step in range(n_chan):
            origin = lax.rem(chan + n_chan - step, n_chan)
            if step:
                arrival(2 * j, origin).wait_recv()
            else:
                pl.when(j == 0)(keep.wait)
                pl.when(j != 0)(arrival(2 * j, origin).wait_recv)
            if turn < hops:
                passed(turn, step).start()

    for turn in range(hops):
        for step in range(n_chan):
            arrival(2 * turn + 1, lax.rem(chan + step, n_chan)).wait_recv()
            passed(turn, step).wait_send()
    for j in range(hops + 1):
        for step in range(n_chan):
            if j or step:
                direct(j, step, mine.at[0], parts_ref.at[0, 0]).wait_send()


def channelise(samples, n_chan, half):
    inputs, frames_in, _, nfft = samples.shape
    frames = frames_in - TAPS + 1
    tiles = CH_WIN // LANES
    n_1 = nfft // LANES
    consts = tables(nfft, CH_WIN * n_chan // n_1)
    x = samples.reshape(inputs, frames_in, 2, n_1, LANES)
    x = jnp.transpose(x, (0, 1, 3, 2, 4)).reshape(inputs, frames_in, 2 * n_1, LANES)
    piece = (n_chan, inputs, frames, 2, tiles, LANES)
    return pl.pallas_call(
        send_kernel,
        out_shape=jax.ShapeDtypeStruct((half + 1,) + piece, jnp.bfloat16),
        in_specs=[pl.BlockSpec(memory_space=pl.ANY)] * 2 + [pl.BlockSpec(memory_space=pltpu.VMEM)] * 4,
        out_specs=pl.BlockSpec(memory_space=OUT_SPACE),
        scratch_shapes=[
            pltpu.VMEM(x.shape, jnp.bfloat16),
            pltpu.VMEM(consts[0].shape, jnp.float32),
            pltpu.VMEM((2 * n_1, frames * LANES), jnp.float32),
            pltpu.VMEM(piece, jnp.bfloat16),
            pltpu.SemaphoreType.DMA((inputs + 1,)),
            pltpu.SemaphoreType.DMA,
            pltpu.SemaphoreType.DMA((half // 2 + 1, n_chan)),
            pltpu.SemaphoreType.DMA((half // 2, n_chan)),
            pltpu.SemaphoreType.DMA((half + 1, n_chan)),
        ],
        compiler_params=pltpu.CompilerParams(collective_id=0, has_side_effects=True),
        name="channelise",
    )(x, *consts)


def correlate_kernel(keeper_ref, parts_ref, out_ref, own, others, dist, gain):
    step = pl.program_id(0)
    _, n_chan, pieces, frames, _, tiles, _ = parts_ref.shape
    inputs = n_chan * pieces
    slots = parts_ref.shape[0]
    n_stn = keeper_ref.shape[0]

    @pl.when(step == 0)
    def _():
        group = lax.axis_index("stn")
        for s in range(slots):
            dist[s] = 0
            gain[s] = jnp.float32(0.0)

        def place(h, rank):
            kept = keeper_ref[group, h] == 1

            @pl.when(kept & (rank < slots))
            def _():
                dist[rank] = jnp.minimum(lax.rem(group + n_stn - h, n_stn), slots - 1)
                gain[rank] = jnp.float32(1.0 / frames)

            return rank + kept.astype(jnp.int32)

        lax.fori_loop(0, n_stn, place, jnp.int32(0))

        for f in range(frames):
            for p in range(2):
                value = parts_ref[0, :, :, f, p].astype(jnp.float32).reshape(inputs, tiles, LANES)
                own[f, p] = jnp.transpose(value, (1, 0, 2))
                for s in range(slots):
                    value = parts_ref[dist[s], :, :, f, p].astype(jnp.float32) * gain[s]
                    value = value.reshape(inputs, tiles, LANES)
                    others[f, p, s] = jnp.transpose(value, (1, 0, 2))

    for t in range(tiles):
        rows = []
        for i in range(pieces):
            rows.append([
                [jnp.broadcast_to(own[f, p, t, pl.ds(step * pieces + i, 1), :], (inputs, LANES)) for p in range(2)]
                for f in range(frames)
            ])
        for s in range(slots):
            block = [[others[f, p, s, t] for p in range(2)] for f in range(frames)]
            for i in range(pieces):
                real, imag = 0.0, 0.0
                for f in range(frames):
                    a_re, a_im = rows[i][f]
                    b_re, b_im = block[f]
                    real = real + (a_re * b_re + a_im * b_im)
                    imag = imag + (a_im * b_re - a_re * b_im)
                top = slice(s * inputs, (s + 1) * inputs)
                col = slice(t * LANES, (t + 1) * LANES)
                out_ref[i, 0, top, col] = real.astype(jnp.bfloat16)
                out_ref[i, 1, top, col] = imag.astype(jnp.bfloat16)


def correlate(keeper, parts):
    slots, n_chan, pieces, frames, _, tiles, _ = parts.shape
    inputs = n_chan * pieces
    out = pl.pallas_call(
        correlate_kernel,
        out_shape=jax.ShapeDtypeStruct((inputs, 2, slots * inputs, tiles * LANES), jnp.bfloat16),
        grid=(n_chan,),
        in_specs=[
            pl.BlockSpec(memory_space=pltpu.SMEM),
            pl.BlockSpec(parts.shape, lambda t: (0,) * 7),
        ],
        out_specs=pl.BlockSpec((pieces, 2, slots * inputs, tiles * LANES), lambda t: (t, 0, 0, 0)),
        scratch_shapes=[
            pltpu.VMEM((frames, 2, tiles, inputs, LANES), jnp.float32),
            pltpu.VMEM((frames, 2, slots, tiles, inputs, LANES), jnp.float32),
            pltpu.SMEM((slots,), jnp.int32),
            pltpu.SMEM((slots,), jnp.float32),
        ],
        name="correlate",
    )(keeper, parts)
    return jnp.transpose(out, (0, 1, 3, 2))


def per_device(samples, keeper):
    half = lax.axis_size("stn") // 2
    return correlate(keeper, channelise(samples, lax.axis_size("chan"), half))


def solution(mesh):
    placed = (P(("stn", "chan"), None, None, None), P())
    return jax.shard_map(
        per_device,
        mesh=mesh,
        in_specs=placed,
        out_specs=P("stn", None, "chan", None),
        check_vma=False,
    )
```

```python
import math

import jax
import jax.numpy as jnp
import numpy as np
from jax import lax
from jax.experimental import pallas as pl
from jax.experimental.pallas import tpu as pltpu
from jax.sharding import PartitionSpec as P

TAPS = 16
LANES = 128
CH_WIN = 1024
HIGH = lax.Precision.HIGHEST
OUT_SPACE = pl.ANY


def tables(nfft, n_k2):
    n_1 = nfft // LANES
    pos = np.arange(TAPS * nfft, dtype=np.float64)
    window = 0.5 - 0.5 * np.cos(2.0 * np.pi * (pos + 0.5) / (TAPS * nfft))
    taps = np.sinc((pos + 0.5) / nfft - TAPS / 2.0) * window
    taps = np.repeat(taps.reshape(TAPS, n_1, LANES), 2, axis=1)
    k_1 = np.arange(n_1)
    n_2 = np.arange(LANES)
    angle = 2.0 * np.pi * (k_1[:, None] * k_1[None, :] % n_1) / n_1
    cosine, sine = np.cos(angle), np.sin(angle)
    first = np.zeros((2, n_1, n_1, 2))
    first[0, :, :, 0] = cosine
    first[0, :, :, 1] = sine
    first[1, :, :, 0] = -sine
    first[1, :, :, 1] = cosine
    first = first.reshape(2 * n_1, 2 * n_1)
    angle = 2.0 * np.pi * (n_2[:, None] * k_1[None, :] % nfft) / nfft
    scale = 1.0 / math.sqrt(nfft)
    turn_c = np.concatenate([np.cos(angle), np.cos(angle)], axis=1) * scale
    turn_s = np.concatenate([np.sin(angle), -np.sin(angle)], axis=1) * scale
    k_2 = np.concatenate([np.arange(0, n_k2, 2), np.arange(1, n_k2, 2)])
    angle = 2.0 * np.pi * (k_2[:, None] * n_2[None, :] % LANES) / LANES
    second = np.concatenate([np.cos(angle), np.sin(angle)], axis=1)
    return [np.asarray(a, np.float32) for a in (taps, first, turn_c, turn_s, second)]


def filter_rows(x_ref, taps_ref, held, inputs, frames):
    rows = taps_ref.shape[1]
    chunk = 16
    for start in range(0, rows, chunk):
        part = slice(start, start + chunk)
        for i in range(inputs):
            totals = [None] * frames
            for step in range(TAPS + frames - 1):
                value = x_ref[i, step, part, :].astype(jnp.float32)
                for f in range(frames):
                    if 0 <= step - f < TAPS:
                        term = value * taps_ref[step - f, part, :]
                        totals[f] = term if totals[f] is None else totals[f] + term
            for f in range(frames):
                seq = i * frames + f
                held[part, seq * LANES : (seq + 1) * LANES] = totals[f]


def transform(held, first_ref, turn_c_ref, turn_s_ref, second_ref, seqs):
    half = LANES // 2
    stage = jnp.dot(first_ref[...], held[...], precision=HIGH, preferred_element_type=jnp.float32)
    lane = lax.broadcasted_iota(jnp.int32, (LANES, LANES), 1)
    sign = jnp.where(lane < half, 1.0, -1.0)
    tops, lows = [], []
    for seq in range(seqs):
        turned = stage[:, seq * LANES : (seq + 1) * LANES].T
        turned = turned * turn_c_ref[...] + pltpu.roll(turned, half, 1) * turn_s_ref[...]
        tops.append(turned)
        lows.append(pltpu.roll(turned, half, 1) * sign)
    rhs = jnp.concatenate([jnp.concatenate(tops, axis=1), jnp.concatenate(lows, axis=1)], axis=0)
    spectra = jnp.dot(second_ref[...], rhs, precision=HIGH, preferred_element_type=jnp.float32)
    tiles = spectra.shape[0] // 2
    low_lane = lax.broadcasted_iota(jnp.int32, (tiles, LANES), 1) < half
    planes = []
    for seq in range(seqs):
        even = spectra[:tiles, seq * LANES : (seq + 1) * LANES]
        odd = spectra[tiles:, seq * LANES : (seq + 1) * LANES]
        real = jnp.where(low_lane, even, pltpu.roll(odd, half, 1))
        imag = jnp.where(low_lane, pltpu.roll(even, half, 1), odd)
        planes.append((real, imag))
    return planes


def send_kernel(
    x_ref, taps_ref, first_ref, turn_c_ref, turn_s_ref, second_ref, parts_ref, held, mine, here_sem, send_sem, pass_sem, recv_sem
):
    n_chan, inputs, frames, _, tiles, _ = mine.shape
    n_stn = lax.axis_size("stn")
    hops = (parts_ref.shape[0] - 1) // 2
    stn = lax.axis_index("stn")
    chan = lax.axis_index("chan")
    odd = lax.rem(stn, 2)
    pair = stn + 1 - 2 * odd

    barrier = pltpu.get_barrier_semaphore()
    for j in range(hops + 1):
        for step in range(n_chan):
            if j or step:
                there = (lax.rem(stn + n_stn - 2 * j, n_stn), lax.rem(chan + step, n_chan))
                pl.semaphore_signal(barrier, inc=1, device_id=there, device_id_type=pl.DeviceIdType.MESH)
    pl.semaphore_signal(barrier, inc=1, device_id=(pair, chan), device_id_type=pl.DeviceIdType.MESH)

    filter_rows(x_ref, taps_ref, held, inputs, frames)
    planes = transform(held, first_ref, turn_c_ref, turn_s_ref, second_ref, inputs * frames)
    for i in range(inputs):
        for f in range(frames):
            for p in range(2):
                plane = planes[i * frames + f][p].astype(jnp.bfloat16)
                for d in range(n_chan):
                    mine[d, i, f, p] = plane[d * tiles : (d + 1) * tiles]
    pl.semaphore_wait(barrier, (hops + 1) * n_chan)

    def direct(j, step):
        to = lax.rem(chan + step, n_chan)
        return pltpu.make_async_remote_copy(
            src_ref=mine.at[to],
            dst_ref=parts_ref.at[2 * j, chan],
            send_sem=send_sem.at[j, step],
            recv_sem=recv_sem.at[2 * j, chan],
            device_id=(lax.rem(stn + 2 * j, n_stn), to),
            device_id_type=pl.DeviceIdType.MESH,
        )

    def arrival(distance, origin):
        return pltpu.make_async_remote_copy(
            src_ref=mine.at[0],
            dst_ref=parts_ref.at[distance, origin],
            send_sem=send_sem.at[0, 0],
            recv_sem=recv_sem.at[distance, origin],
            device_id=(pair, chan),
            device_id_type=pl.DeviceIdType.MESH,
        )

    def passed(j, step):
        origin = lax.rem(chan + step, n_chan)
        return pltpu.make_async_remote_copy(
            src_ref=parts_ref.at[2 * (j + odd), origin],
            dst_ref=parts_ref.at[2 * j + 1, origin],
            send_sem=pass_sem.at[j, step],
            recv_sem=recv_sem.at[2 * j + 1, origin],
            device_id=(pair, chan),
            device_id_type=pl.DeviceIdType.MESH,
        )

    keep = pltpu.make_async_copy(mine.at[chan], parts_ref.at[0, chan], here_sem)
    keep.start()
    for step in range(n_chan):
        for j in range(hops, -1, -1):
            if j or step:
                direct(j, step).start()
    keep.wait()
    for j in range(hops + 1):
        for step in range(n_chan):
            if j or step:
                arrival(2 * j, lax.rem(chan + n_chan - step, n_chan)).wait_recv()
        first = j == 0
        last = j == hops

        @pl.when(odd == 0)
        def _():
            if not last:
                for step in range(n_chan):
                    passed(j, step).start()

        @pl.when(odd == 1)
        def _():
            if not first:
                for step in range(n_chan):
                    passed(j - 1, step).start()

    for j in range(hops):
        for step in range(n_chan):
            arrival(2 * j + 1, lax.rem(chan + step, n_chan)).wait_recv()
            passed(j, step).wait_send()
    for j in range(hops + 1):
        for step in range(n_chan):
            if j or step:
                direct(j, step).wait_send()


def channelise(samples, n_chan, half):
    inputs, frames_in, _, nfft = samples.shape
    frames = frames_in - TAPS + 1
    tiles = CH_WIN // LANES
    n_1 = nfft // LANES
    consts = tables(nfft, CH_WIN * n_chan // n_1)
    x = samples.reshape(inputs, frames_in, 2, n_1, LANES)
    x = jnp.transpose(x, (0, 1, 3, 2, 4)).reshape(inputs, frames_in, 2 * n_1, LANES)
    piece = (n_chan, inputs, frames, 2, tiles, LANES)
    return pl.pallas_call(
        send_kernel,
        out_shape=jax.ShapeDtypeStruct((half + 1,) + piece, jnp.bfloat16),
        in_specs=[pl.BlockSpec(memory_space=pltpu.VMEM)] * 6,
        out_specs=pl.BlockSpec(memory_space=OUT_SPACE),
        scratch_shapes=[
            pltpu.VMEM((2 * n_1, inputs * frames * LANES), jnp.float32),
            pltpu.VMEM(piece, jnp.bfloat16),
            pltpu.SemaphoreType.DMA,
            pltpu.SemaphoreType.DMA((half // 2 + 1, n_chan)),
            pltpu.SemaphoreType.DMA((half // 2, n_chan)),
            pltpu.SemaphoreType.DMA((half + 1, n_chan)),
        ],
        compiler_params=pltpu.CompilerParams(collective_id=0, has_side_effects=True),
        name="channelise",
    )(x, *consts)


def correlate_kernel(keeper_ref, parts_ref, out_ref, own, others, dist, gain):
    step = pl.program_id(0)
    _, n_chan, pieces, frames, _, tiles, _ = parts_ref.shape
    inputs = n_chan * pieces
    pieces = out_ref.shape[0]
    slots = parts_ref.shape[0]
    n_stn = keeper_ref.shape[0]

    @pl.when(step == 0)
    def _():
        group = lax.axis_index("stn")
        for s in range(slots):
            dist[s] = 0
            gain[s] = jnp.float32(0.0)

        def place(h, rank):
            kept = keeper_ref[group, h] == 1

            @pl.when(kept & (rank < slots))
            def _():
                dist[rank] = jnp.minimum(lax.rem(group + n_stn - h, n_stn), slots - 1)
                gain[rank] = jnp.float32(1.0 / frames)

            return rank + kept.astype(jnp.int32)

        lax.fori_loop(0, n_stn, place, jnp.int32(0))

        for f in range(frames):
            for p in range(2):
                value = parts_ref[0, :, :, f, p].astype(jnp.float32).reshape(inputs, tiles, LANES)
                own[f, p] = jnp.transpose(value, (1, 0, 2))
                for s in range(slots):
                    value = parts_ref[dist[s], :, :, f, p].astype(jnp.float32) * gain[s]
                    value = value.reshape(inputs, tiles, LANES)
                    others[f, p, s] = jnp.transpose(value, (1, 0, 2))

    for t in range(tiles):
        rows = []
        for i in range(pieces):
            rows.append([
                [jnp.broadcast_to(own[f, p, t, pl.ds(step * pieces + i, 1), :], (inputs, LANES)) for p in range(2)]
                for f in range(frames)
            ])
        for s in range(slots):
            block = [[others[f, p, s, t] for p in range(2)] for f in range(frames)]
            for i in range(pieces):
                real, imag = 0.0, 0.0
                for f in range(frames):
                    a_re, a_im = rows[i][f]
                    b_re, b_im = block[f]
                    real = real + (a_re * b_re + a_im * b_im)
                    imag = imag + (a_im * b_re - a_re * b_im)
                top = slice(s * inputs, (s + 1) * inputs)
                col = slice(t * LANES, (t + 1) * LANES)
                out_ref[i, 0, top, col] = real.astype(jnp.bfloat16)
                out_ref[i, 1, top, col] = imag.astype(jnp.bfloat16)


def correlate(keeper, parts):
    slots, n_chan, pieces, frames, _, tiles, _ = parts.shape
    inputs = n_chan * pieces
    out = pl.pallas_call(
        correlate_kernel,
        out_shape=jax.ShapeDtypeStruct((inputs, 2, slots * inputs, tiles * LANES), jnp.bfloat16),
        grid=(2,),
        in_specs=[
            pl.BlockSpec(memory_space=pltpu.SMEM),
            pl.BlockSpec(parts.shape, lambda t: (0,) * 7),
        ],
        out_specs=pl.BlockSpec((inputs // 2, 2, slots * inputs, tiles * LANES), lambda t: (t, 0, 0, 0)),
        scratch_shapes=[
            pltpu.VMEM((frames, 2, tiles, inputs, LANES), jnp.float32),
            pltpu.VMEM((frames, 2, slots, tiles, inputs, LANES), jnp.float32),
            pltpu.SMEM((slots,), jnp.int32),
            pltpu.SMEM((slots,), jnp.float32),
        ],
        name="correlate",
    )(keeper, parts)
    return jnp.transpose(out, (0, 1, 3, 2))


def per_device(samples, keeper):
    half = lax.axis_size("stn") // 2
    return correlate(keeper, channelise(samples, lax.axis_size("chan"), half))


def solution(mesh):
    placed = (P(("stn", "chan"), None, None, None), P())
    return jax.shard_map(
        per_device,
        mesh=mesh,
        in_specs=placed,
        out_specs=P("stn", None, "chan", None),
        check_vma=False,
    )
```
